256 devices in a mesh: img: 64 (over y, z_lo, x, core), slab: 4 (over z_hi).
Axes of the slice: x: 4, y: 4, z: 8 (z_hi: 4, z_lo: 2; z = z_hi * 2 + z_lo), core: 2. Of those that a mesh axis runs over, the one named last changes fastest.
Arguments:
- images: bfloat16 [4096, 32768], P('img'), may hold values from -6 to 6
- references: bfloat16 [2, 128, 32768], P(None, 'slab'), may hold values from -6 to 6
- orientations: int32 [4096, 2, 64], P('img'), may hold values from 0 to 127
- ctf_table: float32 [4096, 64], P('img'), may hold values from -1 to 1
- inv_noise: float32 [4096], P('img'), may hold values from 0.002 to 0.02
- class_weight: float32 [2], replicated, may hold values from 0.2 to 5
Outputs:
- updated_volume: float32 [2, 128, 32768], P(None, 'slab', 'img')
The draws below stay inside these ranges and needn't reach their ends.
All inputs are finite; a program needn't handle non-finite values.
Results may differ from the reference program's by a relative error of at most 0.0065.
Values sent between devices are 32-bit elements; how exact they have to be, the bound alone decides.
A program may use at most 192 MiB of HBM per device.

```python
import math
import jax
import jax.numpy as jnp

BOX = 128
KW = 2
LIST = 64
SHELLS = 64
IMGS = 4096


def with_ends(entries, own_key, low, high):
    longest = entries.shape.index(max(entries.shape))
    spots = []
    for shift in (0, 1):
        where = [jax.random.randint(jax.random.fold_in(own_key, axis), (), 0, length) for axis, length in enumerate(entries.shape)]
        where[longest] = (where[longest] + shift) % entries.shape[longest]
        spots.append(tuple(where))
    return entries.at[spots[0]].set(low).at[spots[1]].set(high)


def block_scale(rng, dims, split, low, largest):
    def one(axis_at, blocks):
        draws = jax.random.uniform(jax.random.fold_in(jax.random.fold_in(rng, 6), axis_at), (blocks,), jnp.float32, low / len(split), largest / len(split))
        return jnp.repeat(jnp.exp(draws), dims[axis_at] // blocks).reshape((-1,) + (1,) * (len(dims) - axis_at - 1))

    factor_of = one(*split[0])
    for cut in split[1:]:
        factor_of = factor_of * one(*cut)
    return factor_of


def centred(own_key, dims, width, most, cuts=(), held_as=jnp.bfloat16):
    level = block_scale(own_key, dims, cuts, -0.22, 0.18) if cuts else 1.0
    values = jax.random.normal(own_key, dims, jnp.float32) * width * level
    return jnp.minimum(jnp.maximum(values, -most), most).astype(held_as)


def setup_inputs(seed: int = 0) -> dict:
    key_list = jax.random.split(jax.random.key(seed), 7)
    images = centred(key_list[0], (IMGS, 2 * BOX * BOX), 1.0, 6.0, ((0, 64),))
    references = centred(key_list[1], (KW, BOX, 2 * BOX * BOX), 1.0, 6.0, ((1, 4),))
    orientations = with_ends(jax.random.randint(key_list[2], (IMGS, KW, LIST), 0, BOX), jax.random.fold_in(key_list[2], 1), 0, BOX - 1).astype(jnp.int32)
    ctf_table = jnp.clip(jax.random.uniform(key_list[3], (IMGS, SHELLS), jnp.float32, -1.0, 1.0) * block_scale(key_list[3], (IMGS, SHELLS), ((0, 64),), -0.4, 0.0), -1.0, 1.0)
    inv_noise = jnp.clip(jnp.exp(math.log(0.02) - 2.30258502 * jax.random.uniform(key_list[4], (IMGS,), jnp.float32) ** block_scale(key_list[4], (IMGS,), ((0, 64),), -0.2, 0.2)), 0.002, 0.02)
    class_weight = jnp.clip(jnp.exp(jax.random.uniform(key_list[5], (KW,), jnp.float32, math.log(0.2), math.log(5.0))), 0.2, 5.0)
    return dict(images=images, references=references, orientations=orientations, ctf_table=ctf_table, inv_noise=inv_noise, class_weight=class_weight)


def shell_index():
    position = jnp.arange(BOX * BOX, dtype=jnp.int32)
    column = position % BOX - BOX // 2
    row_place = position // BOX - BOX // 2
    radius_sq = column * column + row_place * row_place
    levels = jnp.arange(1, SHELLS, dtype=jnp.int32)
    inside = (2 * levels[None, :] * levels[None, :] <= radius_sq[:, None]).astype(jnp.int32)
    return jnp.sum(inside, axis=1).astype(jnp.int32)


def reference(images, references, orientations, ctf_table, inv_noise, class_weight):
    shell = shell_index()
    ctf_pixel = ctf_table[:, shell]
    weighted = (images.astype(jnp.float32) * jnp.repeat(ctf_pixel, 2, axis=1)).astype(jnp.bfloat16)
    ctf_square = (ctf_pixel * ctf_pixel).astype(jnp.bfloat16)
    planes = references.reshape(KW * BOX, 2 * BOX * BOX)
    spread = references.astype(jnp.float32).reshape(KW * BOX, BOX * BOX, 2)
    power = jnp.sum(spread * spread, axis=2).astype(jnp.bfloat16)
    intersection = jnp.dot(weighted, planes.T, preferred_element_type=jnp.float32)
    energy = jnp.dot(ctf_square, power.T, preferred_element_type=jnp.float32)
    total_images = images.shape[0]
    table = (2.0 * intersection - energy).reshape(total_images, KW, BOX)
    picked = jnp.take_along_axis(table, orientations, axis=2)
    scores = jnp.log(class_weight)[None, :, None] + inv_noise[:, None, None] * picked
    peak = jnp.max(scores, axis=(1, 2), keepdims=True)
    expo = jnp.exp(scores - peak)
    resp = expo / jnp.sum(expo, axis=(1, 2), keepdims=True)
    image_ids = jnp.arange(total_images, dtype=jnp.int32)[:, None, None]
    class_ids = jnp.arange(KW, dtype=jnp.int32)[None, :, None]
    per_plane = jnp.zeros((total_images, KW, BOX), jnp.float32).at[image_ids, class_ids, orientations].add(resp)
    flat_plane = per_plane.astype(jnp.bfloat16).reshape(total_images, KW * BOX)
    numerator = jnp.dot(flat_plane.T, weighted, preferred_element_type=jnp.float32)
    weight_sum = jnp.dot(flat_plane.T, ctf_square, preferred_element_type=jnp.float32)
    updated = numerator / (jnp.repeat(weight_sum, 2, axis=1) + 1.0)
    return updated.reshape(KW, BOX, 2 * BOX * BOX)
```

```python
import functools

import jax
import jax.numpy as jnp
from jax import lax
from jax.experimental import pallas as pl
from jax.experimental.pallas import tpu as pltpu
from jax.sharding import PartitionSpec as P

BOX = 128
SHELLS = 64
KP = 64
IMG = 64
WIDTH = 32768
BLOCK = 512
CHUNK = 4096
STEPS = WIDTH // CHUNK
PER_STEP = CHUNK // (2 * BLOCK)
ROWS = 8
UNITS = KP // 2 // ROWS
HALF = 256
LOWEST = -3.0e38
MESH = pl.DeviceIdType.MESH
F32 = jnp.float32
BF16 = jnp.bfloat16


def lanes(table, index):
    return jnp.take_along_axis(table, index, axis=1, mode="promise_in_bounds")


def flat(core, x, z, y):
    return ((y * 2 + z) * 4 + x) * 2 + core


def kernel(
    img_hbm, ref_hbm, orient_ref, ctf_ref, noise_ref, prior_ref, out_ref,
    img_v, ref_v, wall, w_send, w_recv, ctf_other, stat_send, stat_own, stat_other, pair_recv,
    part_a, part_b, part_c, fwd_a, dir_a, sum_a, fwd_b, dir_b, sum_b, z_recv,
    tot, tot_recv, counts,
    img_sem, ref_sem, w_ssem, w_rsem, s_ssem, s_rsem, a_ssem, a_rsem, b_ssem, b_rsem, t_ssem, t_rsem,
):
    mine = lax.axis_index("img")
    slab = lax.axis_index("slab")
    core, x = mine % 2, (mine // 2) % 4
    z, y = (mine // 8) % 2, mine // 16

    def at_x(d):
        return (flat(core, (x + d) % 4, z, y), slab)

    def at_y(d):
        return (flat(core, x, z, (y + d) % 4), slab)

    at_z = (flat(core, x, 1 - z, y), slab)
    sibling = (flat(1 - core, x, z, y), slab)

    loads = []
    for g in range(STEPS):
        span = pl.ds(g * CHUNK, CHUNK)
        loads.append(pltpu.make_async_copy(img_hbm.at[:, span], img_v.at[g], img_sem.at[g]))
        loads.append(pltpu.make_async_copy(ref_hbm.at[:, span], ref_v.at[g], ref_sem.at[g]))
    for load in loads:
        load.start()

    peers = [sibling, at_z]
    peers += [at_x(d) for d in (1, 2, 3)] + [at_y(d) for d in (1, 2, 3)]
    for d in (1, 2, 3):
        peers.append((mine, (slab + d) % 4))
        peers.append((flat(1 - core, x, z, y), (slab + d) % 4))
    barrier = pltpu.get_barrier_semaphore()
    for peer in peers:
        pl.semaphore_signal(barrier, inc=1, device_id=peer, device_id_type=MESH)

    own = jnp.concatenate([orient_ref[:, 0, :], orient_ref[:, 1, :]], axis=1).astype(F32)
    own = jnp.transpose(own) - (slab * 32).astype(F32)
    for k in range(2):
        listed = own[k * 64:(k + 1) * 64]
        for p in range(32):
            hit = jnp.where(listed == float(p), 1.0, 0.0)
            counts[k * 32 + p:k * 32 + p + 1, :] = jnp.sum(hit, axis=0, keepdims=True)

    pl.semaphore_wait(barrier, len(peers))

    used = {"a": 0, "b": 0, "s": 0, "t": 0}
    sems = {"a": (a_ssem, a_rsem), "b": (b_ssem, b_rsem), "s": (s_ssem, s_rsem), "t": (t_ssem, t_rsem)}
    sent = []

    def send(kind, src, dst, peer):
        n = used[kind]
        used[kind] = n + 1
        copy = pltpu.make_async_remote_copy(
            src_ref=src, dst_ref=dst, send_sem=sems[kind][0].at[n], recv_sem=sems[kind][1].at[n],
            device_id=peer, device_id_type=MESH,
        )
        copy.start()
        sent.append(copy)
        return copy

    ctf_copy = send("s", ctf_ref, ctf_other, sibling)

    table = jnp.concatenate([ctf_ref[...], jnp.zeros((IMG, 64), F32)], axis=1)
    lane = lax.broadcasted_iota(jnp.int32, (8, 128), 1)
    near = (lane // 2 - 64).astype(F32)
    far = (lane // 2).astype(F32)
    squares = (0.5 * near * near + 0.25, 0.5 * far * far + 0.25)
    even = lax.broadcasted_iota(jnp.int32, (KP, 128), 1) % 2 == 0

    def shells(column, b):
        row = (column + b * 128) // 256 - 64
        radius = squares[b % 2] + 0.5 * (row * row).astype(F32)
        return jnp.minimum(jnp.sqrt(radius), 63.0).astype(jnp.int32)

    def w_copy(g):
        span = pl.ds(g * PER_STEP, PER_STEP)
        return pltpu.make_async_remote_copy(
            src_ref=w_send.at[span], dst_ref=w_recv.at[span], send_sem=w_ssem.at[g], recv_sem=w_rsem.at[g],
            device_id=sibling, device_id_type=MESH,
        )

    def score(g, carry):
        fit, energy = carry
        pltpu.make_async_copy(img_hbm.at[:, pl.ds(0, CHUNK)], img_v.at[g], img_sem.at[g]).wait()
        pltpu.make_async_copy(ref_hbm.at[:, pl.ds(0, CHUNK)], ref_v.at[g], ref_sem.at[g]).wait()
        for other in (True, False):
            part = 1 - core if other else core
            for n in range(PER_STEP):
                inner = pl.multiple_of(n * 2 * BLOCK + part * BLOCK, BLOCK)
                pixels = img_v[g, :, pl.ds(inner, BLOCK)]
                entries = ref_v[g, :, pl.ds(inner, BLOCK)]
                ws, cs, ps = [], [], []
                for b in range(BLOCK // 128):
                    cut = slice(b * 128, (b + 1) * 128)
                    index = jnp.concatenate([shells(g * CHUNK + inner, b)] * 8, axis=0)
                    ctf = lanes(table, index)
                    ws.append((pixels[:, cut].astype(F32) * ctf).astype(BF16))
                    cs.append((ctf * ctf).astype(BF16))
                    wide = entries[:, cut].astype(F32)
                    wide = wide * wide
                    both = wide + pltpu.roll(wide, 127, 1)
                    ps.append(jnp.where(even, both, 0.0).astype(BF16))
                w = jnp.concatenate(ws, axis=1)
                c = jnp.concatenate(cs, axis=1)
                p = jnp.concatenate(ps, axis=1)
                fit = fit + lax.dot_general(entries, w, (((1,), (1,)), ((), ())), preferred_element_type=F32)
                energy = energy + lax.dot_general(p, c, (((1,), (1,)), ((), ())), preferred_element_type=F32)
                t = g * PER_STEP + n
                if other:
                    w_send[t] = w.astype(F32)
                else:
                    wall[t, 0:IMG, :] = w
            if other:
                w_copy(g).start()
        return fit, energy

    zero = jnp.zeros((KP, IMG), F32)
    fit, energy = lax.fori_loop(0, STEPS, score, (zero, zero))

    upper = lax.broadcasted_iota(jnp.int32, (KP, IMG), 0) < 32
    prior = jnp.log(jnp.where(upper, prior_ref[0], prior_ref[1]))
    value = prior + noise_ref[...] * (2.0 * fit - energy)
    count = counts[...]
    listed = count > 0.0
    peak = jnp.max(jnp.where(listed, value, LOWEST), axis=0, keepdims=True)
    weight = jnp.where(listed, count * jnp.exp(value - peak), 0.0)
    mass = jnp.sum(weight, axis=0, keepdims=True)
    stat_send[0:KP, 0:IMG] = weight
    stat_send[KP:KP + 1, 0:IMG] = peak
    stat_send[KP + 1:KP + 2, 0:IMG] = mass
    stats = stat_send.at[pl.ds(KP, 8), :]
    waits = []
    for d in (1, 2, 3):
        waits.append(send("s", stats, stat_own.at[d - 1], (mine, (slab + d) % 4)))
        waits.append(send("s", stats, stat_other.at[d - 1], (flat(1 - core, x, z, y), (slab + d) % 4)))
    waits.append(send("s", stat_send, pair_recv, sibling))

    def widen(g, carry):
        w_copy(g).wait()
        for n in range(PER_STEP):
            t = g * PER_STEP + n
            wall[t, IMG:2 * IMG, :] = w_recv[t].astype(BF16)
        return carry

    lax.fori_loop(0, STEPS, widen, 0)
    ctf_copy.wait_recv()
    squared = jnp.concatenate([ctf_ref[...], ctf_other[...]], axis=0)
    squared = (squared * squared).astype(BF16)
    for copy in waits:
        copy.wait_recv()

    def share(first, second, rest):
        top = first
        for d in range(3):
            top = jnp.maximum(top, rest[d, 0:1, 0:IMG])
        total = second * jnp.exp(first - top)
        for d in range(3):
            total = total + rest[d, 1:2, 0:IMG] * jnp.exp(rest[d, 0:1, 0:IMG] - top)
        return jnp.exp(first - top) / total

    here = weight * share(peak, mass, stat_own)
    there = pair_recv[0:KP, 0:IMG] * share(pair_recv[KP:KP + 1, 0:IMG], pair_recv[KP + 1:KP + 2, 0:IMG], stat_other)
    planes = jnp.concatenate([here, there], axis=1).astype(BF16)

    shell_sum = jnp.dot(planes, squared, preferred_element_type=F32)
    tot[0] = jnp.concatenate([shell_sum[0:32], shell_sum[32:64]], axis=1)
    tot_x = [send("t", tot.at[0], tot_recv.at[d - 1], at_x(d)) for d in (1, 2, 3)]

    def block(dx, dy, dz):
        t = (((y + dy) % 4) * 2 + (z + dz) % 2) * 4 + (x + dx) % 4
        got = jnp.dot(planes, wall[t], preferred_element_type=F32)
        for h in range(2):
            cut = slice(h * HALF, (h + 1) * HALF)
            for u in range(UNITS):
                part_a[0, u, h, dx, dy, dz] = got[u * ROWS:(u + 1) * ROWS, cut]
                low = (UNITS + u) * ROWS
                part_a[1, u, h, dy, dx, dz] = got[low:low + ROWS, cut]

    at = (at_x, at_y)
    units = [(o, u) for u in range(UNITS) for o in range(2)]
    f_a, g_a, h_a, f_b, g_b, h_b, z_c = {}, {}, {}, {}, {}, {}, {}

    def first_a(o, u):
        f_a[o, u] = [
            send("a", part_a.at[o, u, 0, 2], fwd_a.at[o, u, 0], at[o](1)),
            send("a", part_a.at[o, u, 1, 2], fwd_a.at[o, u, 1], at[o](3)),
        ]

    def direct_a(o, u):
        g_a[o, u] = [
            send("a", part_a.at[o, u, 1, 1], dir_a.at[o, u, 1], at[o](1)),
            send("a", part_a.at[o, u, 0, 3], dir_a.at[o, u, 0], at[o](3)),
        ]

    def second_a(o, u):
        h_a[o, u] = []
        for h, d in ((0, 1), (1, 3)):
            f_a[o, u][h].wait_recv()
            part_a[o, u, h, d] = part_a[o, u, h, d] + fwd_a[o, u, h]
            h_a[o, u].append(send("a", part_a.at[o, u, h, d], sum_a.at[o, u, h], at[o](d)))

    def last_a(o, u):
        for h in range(2):
            g_a[o, u][1 - h].wait_recv()
            h_a[o, u][h].wait_recv()
            part_b[o, u, h] = part_a[o, u, h, 0] + dir_a[o, u, h] + sum_a[o, u, h]

    def first_b(o, u):
        to = at[1 - o]
        f_b[o, u] = [
            send("b", part_b.at[o, u, 0, 2], fwd_b.at[o, u, 0], to(1)),
            send("b", part_b.at[o, u, 1, 2], fwd_b.at[o, u, 1], to(3)),
        ]
        g_b[o, u] = [
            send("b", part_b.at[o, u, 1, 1], dir_b.at[o, u, 1], to(1)),
            send("b", part_b.at[o, u, 0, 3], dir_b.at[o, u, 0], to(3)),
        ]

    def second_b(o, u):
        to = at[1 - o]
        h_b[o, u] = []
        for h, d in ((0, 1), (1, 3)):
            f_b[o, u][h].wait_recv()
            part_b[o, u, h, d] = part_b[o, u, h, d] + fwd_b[o, u, h]
            h_b[o, u].append(send("b", part_b.at[o, u, h, d], sum_b.at[o, u, h], to(d)))

    def last_b(o, u):
        for h in range(2):
            g_b[o, u][1 - h].wait_recv()
            h_b[o, u][h].wait_recv()
            done = part_b[o, u, h, 0] + dir_b[o, u, h] + sum_b[o, u, h]
            for dz in range(2):
                part_c[o, u, dz, h] = done[dz]
        z_c[o, u] = send("b", part_c.at[o, u, 1], z_recv.at[o, u], at_z)

    for dy in (2, 1, 3, 0):
        for dz in range(2):
            block(2, dy, dz)
    for u in range(UNITS):
        first_a(0, u)
    for dx in (1, 3, 0):
        for dz in range(2):
            block(dx, 2, dz)
    for u in range(UNITS):
        first_a(1, u)
    for dx in (1, 3, 0):
        for dy in (1, 3, 0):
            for dz in range(2):
                block(dx, dy, dz)
    for o, u in units:
        direct_a(o, u)

    for copy in tot_x:
        copy.wait_recv()
    tot[1] = tot[0] + tot_recv[0] + tot_recv[1] + tot_recv[2]
    tot_y = [send("t", tot.at[1], tot_recv.at[d + 2], at_y(d)) for d in (1, 2, 3)]

    for o, u in units:
        second_a(o, u)
    for copy in tot_y:
        copy.wait_recv()
    tot[2] = tot[1] + tot_recv[3] + tot_recv[4] + tot_recv[5]
    tot_z = send("t", tot.at[2], tot_recv.at[6], at_z)

    for o, u in units:
        last_a(o, u)
        first_b(o, u)
    for o, u in units:
        second_b(o, u)
    tot_z.wait_recv()
    whole = tot[2] + tot_recv[6]
    divisors = []
    blank = jnp.zeros((32, 64), F32)
    for k in range(2):
        table_k = jnp.concatenate([whole[:, k * 64:(k + 1) * 64], blank], axis=1)
        columns = []
        for b in range(BLOCK // 128):
            index = jnp.concatenate([shells(mine * BLOCK, b)] * 4, axis=0)
            columns.append(lanes(table_k, index) + 1.0)
        divisors.append(columns)
    for o, u in units:
        last_b(o, u)
    for o, u in units:
        z_c[o, u].wait_recv()
        for h in range(2):
            done = part_c[o, u, 0, h] + z_recv[o, u, h]
            for b in range(2):
                low = (o * UNITS + u) * ROWS
                below = divisors[o][2 * h + b][u * ROWS:(u + 1) * ROWS]
                out_ref[low:low + ROWS, pl.ds(h * HALF + b * 128, 128)] = done[:, b * 128:(b + 1) * 128] / below

    for copy in sent:
        copy.wait_send()


def shards(images, references, orientations, ctf_table, inv_noise, class_weight):
    classes, planes, width = references.shape
    vmem = pl.BlockSpec(memory_space=pltpu.VMEM)
    hbm = pl.BlockSpec(memory_space=pl.ANY)
    dma = pltpu.SemaphoreType.DMA
    blocks = WIDTH // (2 * BLOCK)
    out = pl.pallas_call(
        kernel,
        out_shape=jax.ShapeDtypeStruct((KP, BLOCK), F32),
        in_specs=[hbm, hbm, vmem, vmem, vmem, pl.BlockSpec(memory_space=pltpu.SMEM)],
        out_specs=vmem,
        scratch_shapes=[
            pltpu.VMEM((STEPS, IMG, CHUNK), BF16),
            pltpu.VMEM((STEPS, KP, CHUNK), BF16),
            pltpu.VMEM((blocks, 2 * IMG, BLOCK), BF16),
            pltpu.VMEM((blocks, IMG, BLOCK), F32),
            pltpu.VMEM((blocks, IMG, BLOCK), F32),
            pltpu.VMEM((IMG, SHELLS), F32),
            pltpu.VMEM((KP + 8, 128), F32),
            pltpu.VMEM((3, 8, 128), F32),
            pltpu.VMEM((3, 8, 128), F32),
            pltpu.VMEM((KP + 8, 128), F32),
            pltpu.VMEM((2, UNITS, 2, 4, 4, 2, ROWS, HALF), F32),
            pltpu.VMEM((2, UNITS, 2, 4, 2, ROWS, HALF), F32),
            pltpu.VMEM((2, UNITS, 2, 2, ROWS, HALF), F32),
            pltpu.VMEM((2, UNITS, 2, 4, 2, ROWS, HALF), F32),
            pltpu.VMEM((2, UNITS, 2, 4, 2, ROWS, HALF), F32),
            pltpu.VMEM((2, UNITS, 2, 4, 2, ROWS, HALF), F32),
            pltpu.VMEM((2, UNITS, 2, 2, ROWS, HALF), F32),
            pltpu.VMEM((2, UNITS, 2, 2, ROWS, HALF), F32),
            pltpu.VMEM((2, UNITS, 2, 2, ROWS, HALF), F32),
            pltpu.VMEM((2, UNITS, 2, ROWS, HALF), F32),
            pltpu.VMEM((3, 32, 128), F32),
            pltpu.VMEM((7, 32, 128), F32),
            pltpu.VMEM((KP, IMG), F32),
            dma((STEPS,)), dma((STEPS,)), dma((STEPS,)), dma((STEPS,)),
            dma((8,)), dma((8,)),
            dma((12 * UNITS,)), dma((12 * UNITS,)),
            dma((14 * UNITS,)), dma((14 * UNITS,)),
            dma((7,)), dma((7,)),
        ],
        compiler_params=pltpu.CompilerParams(
            collective_id=0, has_side_effects=True, vmem_limit_bytes=60 * 2**20
        ),
        name="em_step",
    )(
        images,
        references.reshape(classes * planes, width),
        orientations,
        ctf_table,
        inv_noise.reshape(1, IMG),
        class_weight,
    )
    return out.reshape(classes, planes, BLOCK)


def solution(mesh):
    return jax.shard_map(
        shards,
        mesh=mesh,
        in_specs=(
            P("img", None),
            P(None, "slab", None),
            P("img", None, None),
            P("img", None),
            P("img"),
            P(),
        ),
        out_specs=P(None, "slab", "img"),
        check_vma=False,
    )
```

```python
import functools

import jax
import jax.numpy as jnp
from jax import lax
from jax.experimental import pallas as pl
from jax.experimental.pallas import tpu as pltpu
from jax.sharding import PartitionSpec as P

BOX = 128
SHELLS = 64
KP = 64
IMG = 64
WIDTH = 32768
BLOCK = 512
OWNERS = WIDTH // (2 * BLOCK)
PAIR = 2048
PAIRS = WIDTH // PAIR
ROWS = 8
UNITS = 3
COPIES = 144
HALF = 256
LOWEST = -3.0e38
MESH = pl.DeviceIdType.MESH
F32 = jnp.float32
BF16 = jnp.bfloat16


def lanes(table, index):
    return jnp.take_along_axis(table, index, axis=1, mode="promise_in_bounds")


def flat(core, x, z, y):
    return ((y * 2 + z) * 4 + x) * 2 + core


def kernel(
    img_hbm, ref_hbm, orient_ref, ctf_ref, noise_ref, prior_ref, out_ref,
    img_v, ref_v, near_w, w_send, w_recv, ctf_a, square_a, ctf_b, square_b, ctf_send, ctf_other,
    stat_send, stat_own, stat_other, pair_recv,
    part_a, fwd_a, dir_a, sum_a, part_b, fwd_b, dir_b, sum_b, part_c, z_recv,
    part_q, q_z, q_fwd, q_dir, q_sum, q_b, q_recv,
    tot, tot_recv, counts,
    img_sem, ref_sem, w_ssem, w_rsem, ssem, rsem,
):
    mine = lax.axis_index("img")
    slab = lax.axis_index("slab")
    core, x = mine % 2, (mine // 2) % 4
    z, y = (mine // 8) % 2, mine // 16

    def at_x(d):
        return (flat(core, (x + d) % 4, z, y), slab)

    def at_y(d):
        return (flat(core, x, z, (y + d) % 4), slab)

    at = (at_x, at_y)
    at_z = (flat(core, x, 1 - z, y), slab)
    sibling = (flat(1 - core, x, z, y), slab)

    peers = [sibling, at_z]
    peers += [at_x(d) for d in (1, 2, 3)] + [at_y(d) for d in (1, 2, 3)]
    for d in (1, 2, 3):
        peers.append((mine, (slab + d) % 4))
        peers.append((flat(1 - core, x, z, y), (slab + d) % 4))
    barrier = pltpu.get_barrier_semaphore()
    for peer in peers:
        pl.semaphore_signal(barrier, inc=1, device_id=peer, device_id_type=MESH)

    def load(pair):
        span = pl.ds(pl.multiple_of(pair * PAIR, PAIR), PAIR)
        return (
            pltpu.make_async_copy(img_hbm.at[:, span], img_v.at[pair], img_sem.at[pair]),
            pltpu.make_async_copy(ref_hbm.at[:, span], ref_v.at[pair], ref_sem.at[pair]),
        )

    for g in range(PAIRS // 2):
        for pair in (PAIRS // 2 + g, PAIRS // 2 - 1 - g):
            for copy in load(pair):
                copy.start()

    own = jnp.concatenate([orient_ref[:, 0, :], orient_ref[:, 1, :]], axis=1).astype(F32)
    own = jnp.transpose(own) - (slab * 32).astype(F32)
    for k in range(2):
        listed = own[k * 64:(k + 1) * 64]
        for p in range(32):
            hit = jnp.where(listed == float(p), 1.0, 0.0)
            counts[k * 32 + p:k * 32 + p + 1, :] = jnp.sum(hit, axis=0, keepdims=True)

    table = jnp.concatenate([ctf_ref[...], jnp.zeros((IMG, 64), F32)], axis=1)
    ctf_send[...] = table
    lane = lax.broadcasted_iota(jnp.int32, (8, 128), 1)
    near = (lane // 2 - 64).astype(F32)
    far = (lane // 2).astype(F32)
    squares = (0.5 * near * near + 0.25, 0.5 * far * far + 0.25)

    def shells(row, b):
        radius = squares[b % 2] + 0.5 * (row * row).astype(F32)
        return jnp.minimum(jnp.sqrt(radius), 63.0).astype(jnp.int32)

    def spread(slot, first, start):
        ctf_rows, square_rows = slot
        for k in range(start, 9):
            for b in range(2):
                cut = slice(b * 128, (b + 1) * 128)
                index = jnp.concatenate([shells(first + k, b)] * 8, axis=0)
                ctf = lanes(table, index)
                ctf_rows[k, :, cut] = ctf
                square_rows[k, :, cut] = (ctf * ctf * -0.5).astype(BF16)

    def follow(slot, last, first):
        slot[0][0] = last[0][8]
        slot[1][0] = last[1][8]
        spread(slot, first, 1)

    def last_dims(left, right):
        return lax.dot_general(left, right, (((1,), (1,)), ((), ())), preferred_element_type=F32)

    def score(g, slot, fit):
        ctf_rows, square_rows = slot
        high, low = PAIRS // 2 + g, PAIRS // 2 - 1 - g
        for m in range(0, 9, 3):
            powers, squares_here = [], []
            for k in range(m, m + 3):
                power = None
                if k < 8:
                    entries = ref_v[high, :, k * 256:(k + 1) * 256].astype(F32)
                    power = entries * entries
                if k > 0:
                    entries = ref_v[low, :, (8 - k) * 256:(9 - k) * 256].astype(F32)
                    power = entries * entries if power is None else power + entries * entries
                powers.append(power.astype(BF16))
                squares_here.append(square_rows[k])
            fit = fit + last_dims(jnp.concatenate(powers, axis=1), jnp.concatenate(squares_here, axis=1))
        for pair, mirrored in ((high, False), (low, True)):
            for n in range(2):
                t = pair * 2 + n
                for other in (True, False):
                    part = 1 - core if other else core
                    inner = pl.multiple_of(n * 2 * BLOCK + part * BLOCK, BLOCK)
                    pixels = img_v[pair, :, pl.ds(inner, BLOCK)]
                    entries = ref_v[pair, :, pl.ds(inner, BLOCK)]
                    ws = []
                    for e in range(2):
                        k = 4 * n + 2 * part + e
                        k = 8 - k if mirrored else k
                        ws.append((pixels[:, e * 256:(e + 1) * 256].astype(F32) * ctf_rows[k]).astype(BF16))
                    w = jnp.concatenate(ws, axis=1)
                    fit = fit + last_dims(entries, w)
                    if other:
                        w_send[t] = w.astype(F32)
                    else:
                        near_w[t] = w
        return fit

    def twice(i, fit):
        for g in (2 * i, 2 * i + 1):
            for pair in (PAIRS // 2 + g, PAIRS // 2 - 1 - g):
                for copy in load(pair):
                    copy.wait()
        follow(slot_b, slot_a, i * 16 + 8)
        fit = score(2 * i, slot_a, fit)
        follow(slot_a, slot_b, i * 16 + 16)
        return score(2 * i + 1, slot_b, fit)

    slot_a, slot_b = (ctf_a, square_a), (ctf_b, square_b)
    spread(slot_a, jnp.int32(0), 0)
    fit = lax.fori_loop(0, PAIRS // 4, twice, jnp.zeros((KP, IMG), F32))

    upper = lax.broadcasted_iota(jnp.int32, (KP, IMG), 0) < 32
    prior = jnp.log(jnp.where(upper, prior_ref[0], prior_ref[1]))
    value = prior + noise_ref[...] * (2.0 * fit)
    count = counts[...]
    listed = count > 0.0
    peak = jnp.max(jnp.where(listed, value, LOWEST), axis=0, keepdims=True)
    weight = jnp.where(listed, count * jnp.exp(value - peak), 0.0)
    mass = jnp.sum(weight, axis=0, keepdims=True)
    stat_send[0:KP, 0:IMG] = weight
    stat_send[KP:KP + 1, 0:IMG] = peak
    stat_send[KP + 1:KP + 2, 0:IMG] = mass

    pl.semaphore_wait(barrier, len(peers))

    sent = []

    def send(src, dst, peer):
        n = len(sent)
        copy = pltpu.make_async_remote_copy(
            src_ref=src, dst_ref=dst, send_sem=ssem.at[n], recv_sem=rsem.at[n],
            device_id=peer, device_id_type=MESH,
        )
        copy.start()
        sent.append(copy)
        return copy

    stats = stat_send.at[pl.ds(KP, 8), :]
    waits = []
    for d in (2, 1, 3):
        waits.append(send(stats, stat_own.at[d - 1], (mine, (slab + d) % 4)))
        waits.append(send(stats, stat_other.at[d - 1], (flat(1 - core, x, z, y), (slab + d) % 4)))
    waits.append(send(stat_send, pair_recv, sibling))
    ctf_copy = send(ctf_send, ctf_other, sibling)

    order = [(2, dy, dz) for dy in (2, 1, 3, 0) for dz in (1, 0)]
    order += [(dx, 2, dz) for dx in (1, 3, 0) for dz in (1, 0)]
    order += [(dx, dy, 1) for dx in (1, 3, 0) for dy in (1, 3, 0)]
    order += [(dx, dy, 0) for dx in (1, 3, 0) for dy in (1, 3, 0)]

    def owner(dx, dy, dz):
        return (((y + dy) % 4) * 2 + (z + dz) % 2) * 4 + (x + dx) % 4

    w_copies = {}
    for n, place in enumerate(order):
        w_copies[place] = pltpu.make_async_remote_copy(
            src_ref=w_send.at[owner(*place)], dst_ref=w_recv.at[n], send_sem=w_ssem.at[n],
            recv_sem=w_rsem.at[n], device_id=sibling, device_id_type=MESH,
        )
        w_copies[place].start()

    for copy in waits:
        copy.wait_recv()

    def share(first, second, rest):
        top = first
        for d in range(3):
            top = jnp.maximum(top, rest[d, 0:1, 0:IMG])
        total = second * jnp.exp(first - top)
        for d in range(3):
            total = total + rest[d, 1:2, 0:IMG] * jnp.exp(rest[d, 0:1, 0:IMG] - top)
        return jnp.exp(first - top) / total

    here = weight * share(peak, mass, stat_own)
    there = pair_recv[0:KP, 0:IMG] * share(pair_recv[KP:KP + 1, 0:IMG], pair_recv[KP + 1:KP + 2, 0:IMG], stat_other)
    planes = jnp.concatenate([here, there], axis=1).astype(BF16)

    def block(n):
        dx, dy, dz = order[n]
        both = jnp.concatenate([near_w[owner(dx, dy, dz)], w_recv[n].astype(BF16)], axis=0)
        got = jnp.dot(planes, both, preferred_element_type=F32)
        for h in range(2):
            cut = slice(h * HALF, (h + 1) * HALF)
            for o in range(2):
                first, second = (dx, dy) if o == 0 else (dy, dx)
                for u in range(UNITS + 1):
                    row = (o * (UNITS + 1) + u) * ROWS
                    piece = got[row:row + ROWS, cut]
                    if u < UNITS:
                        part_a[o, u, h, first, second, dz] = piece
                    else:
                        part_q[o, dz, h, first, second] = piece

    def blocks(start, stop):
        for n in range(start, stop):
            w_copies[order[n]].wait_recv()
        for n in range(start, stop):
            block(n)

    f_a, g_a, h_a, f_b, g_b, h_b, z_c = {}, {}, {}, {}, {}, {}, {}
    z_q, f_q, g_q, h_q, d_q = {}, {}, {}, {}, {}

    def ahead(part, into, to):
        return [send(part.at[0, 2], into.at[0], to(1)), send(part.at[1, 2], into.at[1], to(3))]

    def direct(part, into, to):
        return [send(part.at[0, 3], into.at[0], to(3)), send(part.at[1, 1], into.at[1], to(1))]

    def onward(part, came, copies, into, to):
        out = []
        for h, d in ((0, 1), (1, 3)):
            copies[h].wait_recv()
            part[h, d] = part[h, d] + came[h]
            out.append(send(part.at[h, d], into.at[h], to(d)))
        return out

    def first_a(o, u):
        f_a[o, u] = ahead(part_a.at[o, u], fwd_a.at[o, u], at[o])

    def direct_a(o, u):
        g_a[o, u] = direct(part_a.at[o, u], dir_a.at[o, u], at[o])

    def second_a(o, u):
        h_a[o, u] = onward(part_a.at[o, u], fwd_a.at[o, u], f_a[o, u], sum_a.at[o, u], at[o])

    def last_a(o, u):
        for h in range(2):
            g_a[o, u][h].wait_recv()
            h_a[o, u][h].wait_recv()
            part_b[o, u, h] = part_a[o, u, h, 0] + dir_a[o, u, h] + sum_a[o, u, h]
        f_b[o, u] = ahead(part_b.at[o, u], fwd_b.at[o, u], at[1 - o])
        g_b[o, u] = direct(part_b.at[o, u], dir_b.at[o, u], at[1 - o])

    def second_b(o, u):
        h_b[o, u] = onward(part_b.at[o, u], fwd_b.at[o, u], f_b[o, u], sum_b.at[o, u], at[1 - o])

    def last_b(o, u):
        for h in range(2):
            g_b[o, u][h].wait_recv()
            h_b[o, u][h].wait_recv()
            done = part_b[o, u, h, 0] + dir_b[o, u, h] + sum_b[o, u, h]
            for dz in range(2):
                part_c[o, u, dz, h] = done[dz]
        z_c[o, u] = send(part_c.at[o, u, 1], z_recv.at[o, u], at_z)

    def first_q(o):
        z_q[o].wait_recv()
        part_q[o, 0] = part_q[o, 0] + q_z[o]
        f_q[o] = ahead(part_q.at[o, 0], q_fwd.at[o], at[o])
        g_q[o] = direct(part_q.at[o, 0], q_dir.at[o], at[o])

    def second_q(o):
        h_q[o] = onward(part_q.at[o, 0], q_fwd.at[o], f_q[o], q_sum.at[o], at[o])

    def last_q(o):
        for h in range(2):
            g_q[o][h].wait_recv()
            h_q[o][h].wait_recv()
            done = part_q[o, 0, h, 0] + q_dir[o, h] + q_sum[o, h]
            for d in range(4):
                q_b[o, d, h] = done[d]
        d_q[o] = [send(q_b.at[o, d], q_recv.at[o, d - 1], at[1 - o](d)) for d in (2, 1, 3)]

    blocks(0, 8)
    for u in range(UNITS):
        first_a(0, u)
    blocks(8, 14)
    for u in range(UNITS):
        first_a(1, u)
    blocks(14, 23)
    for o in range(2):
        z_q[o] = send(part_q.at[o, 1], q_z.at[o], at_z)
    blocks(23, 32)
    for o in range(2):
        direct_a(o, 0)

    ctf_copy.wait_recv()
    squared = jnp.concatenate([ctf_ref[...], ctf_other[:, 0:SHELLS]], axis=0)
    squared = (squared * squared).astype(BF16)
    shell_sum = jnp.dot(planes, squared, preferred_element_type=F32)
    tot[0] = jnp.concatenate([shell_sum[0:32], shell_sum[32:64]], axis=1)
    tot_x = [send(tot.at[0], tot_recv.at[d - 1], at_x(d)) for d in (1, 2, 3)]

    both = (0, 1)
    for u in range(UNITS):
        for o in both:
            second_a(o, u)
        if u + 1 < UNITS:
            for o in both:
                direct_a(o, u + 1)
    for copy in w_copies.values():
        copy.wait_send()
    for copy in tot_x:
        copy.wait_recv()
    tot[1] = tot[0] + tot_recv[0] + tot_recv[1] + tot_recv[2]
    tot_y = [send(tot.at[1], tot_recv.at[d + 2], at_y(d)) for d in (1, 2, 3)]
    first_q(0)
    for o in both:
        last_a(o, 0)
    for o in both:
        last_a(o, 1)
    for copy in tot_y:
        copy.wait_recv()
    tot[2] = tot[1] + tot_recv[3] + tot_recv[4] + tot_recv[5]
    tot_z = send(tot.at[2], tot_recv.at[6], at_z)
    first_q(1)
    for o in both:
        last_a(o, 2)
    for o in both:
        second_b(o, 0)
    second_q(0)
    for o in both:
        second_b(o, 1)
    second_q(1)
    for o in both:
        second_b(o, 2)
    for o in both:
        last_b(o, 0)
    last_q(0)
    for o in both:
        last_b(o, 1)
    last_q(1)
    for o in both:
        last_b(o, 2)
    early = len(sent) - 40
    for copy in sent[:early]:
        copy.wait_send()

    tot_z.wait_recv()
    whole = tot[2] + tot_recv[6]
    divisors = []
    blank = jnp.zeros((32, 64), F32)
    for k in range(2):
        table_k = jnp.concatenate([whole[:, k * 64:(k + 1) * 64], blank], axis=1)
        columns = []
        for b in range(BLOCK // 128):
            row = mine * 2 + b // 2 - 64
            index = jnp.concatenate([shells(row, b)] * 4, axis=0)
            columns.append(lanes(table_k, index) + 1.0)
        divisors.append(columns)

    def finish(o, u, h, done):
        low = (o * (UNITS + 1) + u) * ROWS
        for b in range(2):
            below = divisors[o][2 * h + b][u * ROWS:(u + 1) * ROWS]
            out_ref[low:low + ROWS, pl.ds(h * HALF + b * 128, 128)] = done[:, b * 128:(b + 1) * 128] / below

    for u in range(UNITS):
        for o in range(2):
            z_c[o, u].wait_recv()
            for h in range(2):
                finish(o, u, h, part_c[o, u, 0, h] + z_recv[o, u, h])
    for o in range(2):
        for copy in d_q[o]:
            copy.wait_recv()
        for h in range(2):
            finish(o, UNITS, h, q_b[o, 0, h] + q_recv[o, 0, h] + q_recv[o, 1, h] + q_recv[o, 2, h])

    for copy in sent[early:]:
        copy.wait_send()


def shards(images, references, orientations, ctf_table, inv_noise, class_weight):
    classes, planes, width = references.shape
    vmem = pl.BlockSpec(memory_space=pltpu.VMEM)
    hbm = pl.BlockSpec(memory_space=pl.ANY)
    dma = pltpu.SemaphoreType.DMA
    out = pl.pallas_call(
        kernel,
        out_shape=jax.ShapeDtypeStruct((KP, BLOCK), F32),
        in_specs=[hbm, hbm, vmem, vmem, vmem, pl.BlockSpec(memory_space=pltpu.SMEM)],
        out_specs=vmem,
        scratch_shapes=[
            pltpu.VMEM((PAIRS, IMG, PAIR), BF16),
            pltpu.VMEM((PAIRS, KP, PAIR), BF16),
            pltpu.VMEM((OWNERS, IMG, BLOCK), BF16),
            pltpu.VMEM((OWNERS, IMG, BLOCK), F32),
            pltpu.VMEM((OWNERS, IMG, BLOCK), F32),
            pltpu.VMEM((9, IMG, 256), F32),
            pltpu.VMEM((9, IMG, 256), BF16),
            pltpu.VMEM((9, IMG, 256), F32),
            pltpu.VMEM((9, IMG, 256), BF16),
            pltpu.VMEM((IMG, 128), F32),
            pltpu.VMEM((IMG, 128), F32),
            pltpu.VMEM((KP + 8, 128), F32),
            pltpu.VMEM((3, 8, 128), F32),
            pltpu.VMEM((3, 8, 128), F32),
            pltpu.VMEM((KP + 8, 128), F32),
            pltpu.VMEM((2, UNITS, 2, 4, 4, 2, ROWS, HALF), F32),
            pltpu.VMEM((2, UNITS, 2, 4, 2, ROWS, HALF), F32),
            pltpu.VMEM((2, UNITS, 2, 4, 2, ROWS, HALF), F32),
            pltpu.VMEM((2, UNITS, 2, 4, 2, ROWS, HALF), F32),
            pltpu.VMEM((2, UNITS, 2, 4, 2, ROWS, HALF), F32),
            pltpu.VMEM((2, UNITS, 2, 2, ROWS, HALF), F32),
            pltpu.VMEM((2, UNITS, 2, 2, ROWS, HALF), F32),
            pltpu.VMEM((2, UNITS, 2, 2, ROWS, HALF), F32),
            pltpu.VMEM((2, UNITS, 2, 2, ROWS, HALF), F32),
            pltpu.VMEM((2, UNITS, 2, ROWS, HALF), F32),
            pltpu.VMEM((2, 2, 2, 4, 4, ROWS, HALF), F32),
            pltpu.VMEM((2, 2, 4, 4, ROWS, HALF), F32),
            pltpu.VMEM((2, 2, 4, ROWS, HALF), F32),
            pltpu.VMEM((2, 2, 4, ROWS, HALF), F32),
            pltpu.VMEM((2, 2, 4, ROWS, HALF), F32),
            pltpu.VMEM((2, 4, 2, ROWS, HALF), F32),
            pltpu.VMEM((2, 3, 2, ROWS, HALF), F32),
            pltpu.VMEM((3, 32, 128), F32),
            pltpu.VMEM((7, 32, 128), F32),
            pltpu.VMEM((KP, IMG), F32),
            dma((PAIRS,)), dma((PAIRS,)), dma((OWNERS,)), dma((OWNERS,)), dma((COPIES,)), dma((COPIES,)),
        ],
        compiler_params=pltpu.CompilerParams(
            collective_id=0, has_side_effects=True, vmem_limit_bytes=60 * 2**20
        ),
        name="em_step",
    )(
        images,
        references.reshape(classes * planes, width),
        orientations,
        ctf_table,
        inv_noise.reshape(1, IMG),
        class_weight,
    )
    return out.reshape(classes, planes, BLOCK)


def solution(mesh):
    return jax.shard_map(
        shards,
        mesh=mesh,
        in_specs=(
            P("img", None),
            P(None, "slab", None),
            P("img", None, None),
            P("img", None),
            P("img"),
            P(),
        ),
        out_specs=P(None, "slab", "img"),
        check_vma=False,
    )
```

```python
import functools

import jax
import jax.numpy as jnp
from jax import lax
from jax.experimental import pallas as pl
from jax.experimental.pallas import tpu as pltpu
from jax.sharding import PartitionSpec as P

BOX = 128
SHELLS = 64
KP = 64
IMG = 64
WIDTH = 32768
BLOCK = 512
OWNERS = WIDTH // (2 * BLOCK)
PAIR = 2048
PAIRS = WIDTH // PAIR
ROWS = 8
UNITS = 3
COPIES = 144
HALF = 256
LOWEST = -3.0e38
MESH = pl.DeviceIdType.MESH
F32 = jnp.float32
BF16 = jnp.bfloat16


def lanes(table, index):
    return jnp.take_along_axis(table, index, axis=1, mode="promise_in_bounds")


def flat(core, x, z, y):
    return ((y * 2 + z) * 4 + x) * 2 + core


def kernel(
    img_hbm, ref_hbm, orient_ref, ctf_ref, noise_ref, prior_ref, out_ref,
    img_v, ref_v, near_w, w_send, w_recv, ctf_a, square_a, ctf_b, square_b, ctf_send, ctf_other,
    stat_send, stat_own, stat_other, pair_recv,
    part_a, fwd_a, dir_a, sum_a, part_b, b_recv, z_recv,
    part_q, q_z, q_fwd, q_dir, q_sum, q_b, q_recv,
    tot, tot_recv, counts,
    img_sem, ref_sem, w_ssem, w_rsem, ssem, rsem,
):
    mine = lax.axis_index("img")
    slab = lax.axis_index("slab")
    core, x = mine % 2, (mine // 2) % 4
    z, y = (mine // 8) % 2, mine // 16

    def at_x(d):
        return (flat(core, (x + d) % 4, z, y), slab)

    def at_y(d):
        return (flat(core, x, z, (y + d) % 4), slab)

    at = (at_x, at_y)
    at_z = (flat(core, x, 1 - z, y), slab)
    sibling = (flat(1 - core, x, z, y), slab)

    peers = [sibling, at_z]
    peers += [to(d) for to in at for d in (1, 2, 3)]
    for d in (1, 2, 3):
        peers.append((mine, (slab + d) % 4))
        peers.append((flat(1 - core, x, z, y), (slab + d) % 4))
    barrier = pltpu.get_barrier_semaphore()
    for peer in peers:
        pl.semaphore_signal(barrier, inc=1, device_id=peer, device_id_type=MESH)

    def load(pair):
        span = pl.ds(pl.multiple_of(pair * PAIR, PAIR), PAIR)
        return (
            pltpu.make_async_copy(img_hbm.at[:, span], img_v.at[pair], img_sem.at[pair]),
            pltpu.make_async_copy(ref_hbm.at[:, span], ref_v.at[pair], ref_sem.at[pair]),
        )

    for g in range(PAIRS // 2):
        for pair in (PAIRS // 2 + g, PAIRS // 2 - 1 - g):
            for copy in load(pair):
                copy.start()

    own = jnp.concatenate([orient_ref[:, 0, :], orient_ref[:, 1, :]], axis=1).astype(F32)
    own = jnp.transpose(own) - (slab * 32).astype(F32)
    own = jnp.concatenate([own[0:64], own[64:128]], axis=1)
    for p in range(32):
        hit = jnp.where(own == float(p), 1.0, 0.0)
        counts[p:p + 1, :] = jnp.sum(hit, axis=0, keepdims=True)

    table = jnp.concatenate([ctf_ref[...], jnp.zeros((IMG, 64), F32)], axis=1)
    ctf_send[...] = table
    lane = lax.broadcasted_iota(jnp.int32, (8, 128), 1)
    near = (lane // 2 - 64).astype(F32)
    far = (lane // 2).astype(F32)
    squares = (0.5 * near * near + 0.25, 0.5 * far * far + 0.25)

    def shells(row, b):
        radius = squares[b % 2] + 0.5 * (row * row).astype(F32)
        return jnp.minimum(jnp.sqrt(radius), 63.0).astype(jnp.int32)

    def spread(slot, first, start):
        ctf_rows, square_rows = slot
        for k in range(start, 9):
            for b in range(2):
                cut = slice(b * 128, (b + 1) * 128)
                index = jnp.concatenate([shells(first + k, b)] * 8, axis=0)
                ctf = lanes(table, index)
                ctf_rows[k, :, cut] = ctf
                square_rows[k, :, cut] = (ctf * ctf).astype(BF16)

    def follow(slot, last, first):
        slot[0][0] = last[0][8]
        slot[1][0] = last[1][8]
        spread(slot, first, 1)

    def last_dims(left, right):
        return lax.dot_general(left, right, (((1,), (1,)), ((), ())), preferred_element_type=F32)

    def score(g, slot, sums):
        fit, energy = sums
        ctf_rows, square_rows = slot
        high, low = PAIRS // 2 + g, PAIRS // 2 - 1 - g
        for m in range(0, 9, 3):
            powers, squares_here = [], []
            for k in range(m, m + 3):
                power = None
                if k < 8:
                    entries = ref_v[high, :, k * 256:(k + 1) * 256]
                    power = entries * entries
                if k > 0:
                    entries = ref_v[low, :, (8 - k) * 256:(9 - k) * 256]
                    power = entries * entries if power is None else power + entries * entries
                powers.append(power)
                squares_here.append(square_rows[k])
            energy = energy + last_dims(jnp.concatenate(powers, axis=1), jnp.concatenate(squares_here, axis=1))
        for pair, mirrored in ((high, False), (low, True)):
            for n in range(2):
                t = pair * 2 + n
                for other in (True, False):
                    part = 1 - core if other else core
                    inner = pl.multiple_of(n * 2 * BLOCK + part * BLOCK, BLOCK)
                    pixels = img_v[pair, :, pl.ds(inner, BLOCK)]
                    entries = ref_v[pair, :, pl.ds(inner, BLOCK)]
                    ws = []
                    for e in range(2):
                        k = 4 * n + 2 * part + e
                        k = 8 - k if mirrored else k
                        ws.append((pixels[:, e * 256:(e + 1) * 256].astype(F32) * ctf_rows[k]).astype(BF16))
                    w = jnp.concatenate(ws, axis=1)
                    fit = fit + last_dims(entries, w)
                    if other:
                        w_send[t] = w.astype(F32)
                    else:
                        near_w[t] = w
        return fit, energy

    def twice(i, fit):
        for g in (2 * i, 2 * i + 1):
            for pair in (PAIRS // 2 + g, PAIRS // 2 - 1 - g):
                for copy in load(pair):
                    copy.wait()
        follow(slot_b, slot_a, i * 16 + 8)
        fit = score(2 * i, slot_a, fit)
        follow(slot_a, slot_b, i * 16 + 16)
        return score(2 * i + 1, slot_b, fit)

    slot_a, slot_b = (ctf_a, square_a), (ctf_b, square_b)
    spread(slot_a, jnp.int32(0), 0)
    zero = jnp.zeros((KP, IMG), F32)
    fit, energy = lax.fori_loop(0, PAIRS // 4, twice, (zero, zero))

    upper = lax.broadcasted_iota(jnp.int32, (KP, IMG), 0) < 32
    prior = jnp.log(jnp.where(upper, prior_ref[0], prior_ref[1]))
    value = prior + noise_ref[...] * (2.0 * fit - energy)
    count = jnp.concatenate([counts[:, 0:IMG], counts[:, IMG:2 * IMG]], axis=0)
    listed = count > 0.0
    peak = jnp.max(jnp.where(listed, value, LOWEST), axis=0, keepdims=True)
    weight = jnp.where(listed, count * jnp.exp(value - peak), 0.0)
    mass = jnp.sum(weight, axis=0, keepdims=True)
    stat_send[0:KP, 0:IMG] = weight
    stat_send[KP:KP + 1, 0:IMG] = peak
    stat_send[KP + 1:KP + 2, 0:IMG] = mass

    pl.semaphore_wait(barrier, len(peers))

    sent = []

    def send(src, dst, peer):
        n = len(sent)
        copy = pltpu.make_async_remote_copy(
            src_ref=src, dst_ref=dst, send_sem=ssem.at[n], recv_sem=rsem.at[n],
            device_id=peer, device_id_type=MESH,
        )
        copy.start()
        sent.append(copy)
        return copy

    stats = stat_send.at[pl.ds(KP, 8), :]
    waits = []
    for d in (2, 1, 3):
        waits.append(send(stats, stat_own.at[d - 1], (mine, (slab + d) % 4)))
        waits.append(send(stats, stat_other.at[d - 1], (flat(1 - core, x, z, y), (slab + d) % 4)))
    waits.append(send(stat_send, pair_recv, sibling))
    ctf_copy = send(ctf_send, ctf_other, sibling)

    order = [(2, dy, dz) for dy in (2, 1, 3, 0) for dz in (1, 0)]
    order += [(dx, 2, dz) for dx in (1, 3, 0) for dz in (1, 0)]
    order += [(dx, dy, 1) for dx in (1, 3, 0) for dy in (1, 3, 0)]
    order += [(dx, dy, 0) for dx in (1, 3, 0) for dy in (1, 3, 0)]

    def owner(dx, dy, dz):
        return (((y + dy) % 4) * 2 + (z + dz) % 2) * 4 + (x + dx) % 4

    w_copies = {}
    for n, place in enumerate(order):
        w_copies[place] = pltpu.make_async_remote_copy(
            src_ref=w_send.at[owner(*place)], dst_ref=w_recv.at[n], send_sem=w_ssem.at[n],
            recv_sem=w_rsem.at[n], device_id=sibling, device_id_type=MESH,
        )
        w_copies[place].start()

    for copy in waits:
        copy.wait_recv()

    def share(first, second, rest):
        top = first
        for d in range(3):
            top = jnp.maximum(top, rest[d, 0:1, 0:IMG])
        total = second * jnp.exp(first - top)
        for d in range(3):
            total = total + rest[d, 1:2, 0:IMG] * jnp.exp(rest[d, 0:1, 0:IMG] - top)
        return jnp.exp(first - top) / total

    here = weight * share(peak, mass, stat_own)
    there = pair_recv[0:KP, 0:IMG] * share(pair_recv[KP:KP + 1, 0:IMG], pair_recv[KP + 1:KP + 2, 0:IMG], stat_other)
    planes = jnp.concatenate([here, there], axis=1).astype(BF16)

    def block(n):
        dx, dy, dz = order[n]
        both = jnp.concatenate([near_w[owner(dx, dy, dz)], w_recv[n].astype(BF16)], axis=0)
        got = jnp.dot(planes, both, preferred_element_type=F32)
        for h in range(2):
            cut = slice(h * HALF, (h + 1) * HALF)
            for o in range(2):
                first, second = (dx, dy) if o == 0 else (dy, dx)
                for u in range(UNITS + 1):
                    row = (o * (UNITS + 1) + u) * ROWS
                    piece = got[row:row + ROWS, cut]
                    if u < UNITS:
                        part_a[o, u, h, first, second, dz] = piece
                    else:
                        part_q[o, dz, h, first, second] = piece

    def blocks(start, stop):
        for n in range(start, stop):
            w_copies[order[n]].wait_recv()
        for n in range(start, stop):
            block(n)

    f_a, g_a, h_a, d_b, z_c = {}, {}, {}, {}, {}
    z_q, f_q, g_q, h_q, d_q = {}, {}, {}, {}, {}

    def ahead(part, into, to):
        return [send(part.at[0, 2], into.at[0], to(1)), send(part.at[1, 2], into.at[1], to(3))]

    def direct(part, into, to):
        return [send(part.at[0, 3], into.at[0], to(3)), send(part.at[1, 1], into.at[1], to(1))]

    def onward(part, came, copies, into, to):
        out = []
        for h, d in ((0, 1), (1, 3)):
            copies[h].wait_recv()
            part[h, d] = part[h, d] + came[h]
            out.append(send(part.at[h, d], into.at[h], to(d)))
        return out

    def first_a(o, u):
        f_a[o, u] = ahead(part_a.at[o, u], fwd_a.at[o, u], at[o])

    def direct_a(o, u):
        g_a[o, u] = direct(part_a.at[o, u], dir_a.at[o, u], at[o])

    def second_a(o, u):
        h_a[o, u] = onward(part_a.at[o, u], fwd_a.at[o, u], f_a[o, u], sum_a.at[o, u], at[o])

    def last_a(o, u):
        for h in range(2):
            g_a[o, u][h].wait_recv()
            h_a[o, u][h].wait_recv()
            done = part_a[o, u, h, 0] + dir_a[o, u, h] + sum_a[o, u, h]
            for d in range(4):
                for dz in range(2):
                    part_b[o, u, d, dz, h] = done[d, dz]
        d_b[o, u] = [
            send(part_b.at[o, u, d], b_recv.at[o, u, d - 1], at[1 - o](d)) for d in (2, 1, 3)
        ]

    def last_b(o, u):
        for copy in d_b[o, u]:
            copy.wait_recv()
        part_b[o, u, 0] = part_b[o, u, 0] + b_recv[o, u, 0] + b_recv[o, u, 1] + b_recv[o, u, 2]
        z_c[o, u] = send(part_b.at[o, u, 0, 1], z_recv.at[o, u], at_z)

    def first_q(o):
        z_q[o].wait_recv()
        part_q[o, 0] = part_q[o, 0] + q_z[o]
        f_q[o] = ahead(part_q.at[o, 0], q_fwd.at[o], at[o])
        g_q[o] = direct(part_q.at[o, 0], q_dir.at[o], at[o])

    def second_q(o):
        h_q[o] = onward(part_q.at[o, 0], q_fwd.at[o], f_q[o], q_sum.at[o], at[o])

    def last_q(o):
        for h in range(2):
            g_q[o][h].wait_recv()
            h_q[o][h].wait_recv()
            done = part_q[o, 0, h, 0] + q_dir[o, h] + q_sum[o, h]
            for d in range(4):
                q_b[o, d, h] = done[d]
        d_q[o] = [send(q_b.at[o, d], q_recv.at[o, d - 1], at[1 - o](d)) for d in (2, 1, 3)]

    blocks(0, 8)
    for u in range(UNITS):
        first_a(0, u)
    blocks(8, 14)
    for u in range(UNITS):
        first_a(1, u)
    blocks(14, 23)
    for o in range(2):
        z_q[o] = send(part_q.at[o, 1], q_z.at[o], at_z)
    blocks(23, 32)
    for o in range(2):
        direct_a(o, 0)

    ctf_copy.wait_recv()
    squared = jnp.concatenate([ctf_ref[...], ctf_other[:, 0:SHELLS]], axis=0)
    squared = (squared * squared).astype(BF16)
    shell_sum = jnp.dot(planes, squared, preferred_element_type=F32)
    tot[0] = jnp.concatenate([shell_sum[0:32], shell_sum[32:64]], axis=1)
    tot_x = [send(tot.at[0], tot_recv.at[d - 1], at_x(d)) for d in (1, 2, 3)]

    both = (0, 1)
    for u in range(UNITS):
        for o in both:
            second_a(o, u)
        if u + 1 < UNITS:
            for o in both:
                direct_a(o, u + 1)
    for copy in w_copies.values():
        copy.wait_send()
    for copy in tot_x:
        copy.wait_recv()
    tot[1] = tot[0] + tot_recv[0] + tot_recv[1] + tot_recv[2]
    tot_y = [send(tot.at[1], tot_recv.at[d + 2], at_y(d)) for d in (1, 2, 3)]
    for o in both:
        last_a(o, 0)
    first_q(0)
    for o in both:
        last_a(o, 1)
    for copy in tot_y:
        copy.wait_recv()
    tot[2] = tot[1] + tot_recv[3] + tot_recv[4] + tot_recv[5]
    tot_z = send(tot.at[2], tot_recv.at[6], at_z)
    first_q(1)
    for o in both:
        last_a(o, 2)
    second_q(0)
    for o in both:
        last_b(o, 0)
    second_q(1)
    for o in both:
        last_b(o, 1)
    last_q(0)
    for o in both:
        last_b(o, 2)
    last_q(1)
    early = len(sent) - 40
    for copy in sent[:early]:
        copy.wait_send()

    tot_z.wait_recv()
    whole = tot[2] + tot_recv[6]
    divisors = []
    blank = jnp.zeros((32, 64), F32)
    for k in range(2):
        table_k = jnp.concatenate([whole[:, k * 64:(k + 1) * 64], blank], axis=1)
        columns = []
        for b in range(BLOCK // 128):
            row = mine * 2 + b // 2 - 64
            index = jnp.concatenate([shells(row, b)] * 4, axis=0)
            columns.append(lanes(table_k, index) + 1.0)
        divisors.append(columns)

    def finish(o, u, h, done):
        low = (o * (UNITS + 1) + u) * ROWS
        for b in range(2):
            below = divisors[o][2 * h + b][u * ROWS:(u + 1) * ROWS]
            out_ref[low:low + ROWS, pl.ds(h * HALF + b * 128, 128)] = done[:, b * 128:(b + 1) * 128] / below

    for u in range(UNITS):
        for o in range(2):
            z_c[o, u].wait_recv()
            for h in range(2):
                finish(o, u, h, part_b[o, u, 0, 0, h] + z_recv[o, u, h])
    for o in range(2):
        for copy in d_q[o]:
            copy.wait_recv()
        for h in range(2):
            finish(o, UNITS, h, q_b[o, 0, h] + q_recv[o, 0, h] + q_recv[o, 1, h] + q_recv[o, 2, h])

    for copy in sent[early:]:
        copy.wait_send()


def shards(images, references, orientations, ctf_table, inv_noise, class_weight):
    classes, planes, width = references.shape
    vmem = pl.BlockSpec(memory_space=pltpu.VMEM)
    hbm = pl.BlockSpec(memory_space=pl.ANY)
    dma = pltpu.SemaphoreType.DMA
    out = pl.pallas_call(
        kernel,
        out_shape=pltpu.VMEM((KP, BLOCK), F32),
        in_specs=[hbm, hbm, vmem, vmem, vmem, pl.BlockSpec(memory_space=pltpu.SMEM)],
        out_specs=vmem,
        scratch_shapes=[
            pltpu.VMEM((PAIRS, IMG, PAIR), BF16),
            pltpu.VMEM((PAIRS, KP, PAIR), BF16),
            pltpu.VMEM((OWNERS, IMG, BLOCK), BF16),
            pltpu.VMEM((OWNERS, IMG, BLOCK), F32),
            pltpu.VMEM((OWNERS, IMG, BLOCK), F32),
            pltpu.VMEM((9, IMG, 256), F32),
            pltpu.VMEM((9, IMG, 256), BF16),
            pltpu.VMEM((9, IMG, 256), F32),
            pltpu.VMEM((9, IMG, 256), BF16),
            pltpu.VMEM((IMG, 128), F32),
            pltpu.VMEM((IMG, 128), F32),
            pltpu.VMEM((KP + 8, 128), F32),
            pltpu.VMEM((3, 8, 128), F32),
            pltpu.VMEM((3, 8, 128), F32),
            pltpu.VMEM((KP + 8, 128), F32),
            pltpu.VMEM((2, UNITS, 2, 4, 4, 2, ROWS, HALF), F32),
            pltpu.VMEM((2, UNITS, 2, 4, 2, ROWS, HALF), F32),
            pltpu.VMEM((2, UNITS, 2, 4, 2, ROWS, HALF), F32),
            pltpu.VMEM((2, UNITS, 2, 4, 2, ROWS, HALF), F32),
            pltpu.VMEM((2, UNITS, 4, 2, 2, ROWS, HALF), F32),
            pltpu.VMEM((2, UNITS, 3, 2, 2, ROWS, HALF), F32),
            pltpu.VMEM((2, UNITS, 2, ROWS, HALF), F32),
            pltpu.VMEM((2, 2, 2, 4, 4, ROWS, HALF), F32),
            pltpu.VMEM((2, 2, 4, 4, ROWS, HALF), F32),
            pltpu.VMEM((2, 2, 4, ROWS, HALF), F32),
            pltpu.VMEM((2, 2, 4, ROWS, HALF), F32),
            pltpu.VMEM((2, 2, 4, ROWS, HALF), F32),
            pltpu.VMEM((2, 4, 2, ROWS, HALF), F32),
            pltpu.VMEM((2, 3, 2, ROWS, HALF), F32),
            pltpu.VMEM((3, 32, 128), F32),
            pltpu.VMEM((7, 32, 128), F32),
            pltpu.VMEM((32, 2 * IMG), F32),
            dma((PAIRS,)), dma((PAIRS,)), dma((OWNERS,)), dma((OWNERS,)), dma((COPIES,)), dma((COPIES,)),
        ],
        compiler_params=pltpu.CompilerParams(
            collective_id=0, has_side_effects=True, vmem_limit_bytes=60 * 2**20
        ),
        name="em_step",
    )(
        images,
        references.reshape(classes * planes, width),
        orientations,
        ctf_table,
        inv_noise.reshape(1, IMG),
        class_weight,
    )
    return out.reshape(classes, planes, BLOCK)


def solution(mesh):
    return jax.shard_map(
        shards,
        mesh=mesh,
        in_specs=(
            P("img", None),
            P(None, "slab", None),
            P("img", None, None),
            P("img", None),
            P("img"),
            P(),
        ),
        out_specs=P(None, "slab", "img"),
        check_vma=False,
    )
```

```python
import functools

import jax
import jax.numpy as jnp
from jax import lax
from jax.experimental import pallas as pl
from jax.experimental.pallas import tpu as pltpu
from jax.sharding import PartitionSpec as P

BOX = 128
SHELLS = 64
KP = 64
IMG = 64
WIDTH = 32768
BLOCK = 512
OWNERS = WIDTH // (2 * BLOCK)
PAIR = 2048
PAIRS = WIDTH // PAIR
ROWS = 8
UNITS = 3
COPIES = 144
HALF = 256
LOWEST = -3.0e38
MESH = pl.DeviceIdType.MESH
F32 = jnp.float32
BF16 = jnp.bfloat16


def lanes(table, index):
    return jnp.take_along_axis(table, index, axis=1, mode="promise_in_bounds")


def flat(core, x, z, y):
    return ((y * 2 + z) * 4 + x) * 2 + core


def kernel(
    img_hbm, ref_hbm, orient_ref, ctf_ref, noise_ref, prior_ref, out_ref,
    img_v, ref_v, near_w, w_send, w_recv, ctf_a, square_a, ctf_b, square_b, ctf_send, ctf_other,
    stat_send, stat_own, stat_other, pair_recv,
    part_a, fwd_a, dir_a, sum_a, part_b, b_recv, z_recv,
    part_q, q_z, q_fwd, q_dir, q_sum, q_b, q_recv,
    tot, tot_recv, counts,
    img_sem, ref_sem, w_ssem, w_rsem, ssem, rsem,
):
    mine = lax.axis_index("img")
    slab = lax.axis_index("slab")
    core, x = mine % 2, (mine // 2) % 4
    z, y = (mine // 8) % 2, mine // 16

    def at_x(d):
        return (flat(core, (x + d) % 4, z, y), slab)

    def at_y(d):
        return (flat(core, x, z, (y + d) % 4), slab)

    at = (at_x, at_y)
    at_z = (flat(core, x, 1 - z, y), slab)
    sibling = (flat(1 - core, x, z, y), slab)

    peers = [sibling, at_z]
    peers += [to(d) for to in at for d in (1, 2, 3)]
    for d in (1, 2, 3):
        peers.append((mine, (slab + d) % 4))
        peers.append((flat(1 - core, x, z, y), (slab + d) % 4))
    barrier = pltpu.get_barrier_semaphore()
    for peer in peers:
        pl.semaphore_signal(barrier, inc=1, device_id=peer, device_id_type=MESH)

    def load(pair):
        span = pl.ds(pl.multiple_of(pair * PAIR, PAIR), PAIR)
        return (
            pltpu.make_async_copy(img_hbm.at[:, span], img_v.at[pair], img_sem.at[pair]),
            pltpu.make_async_copy(ref_hbm.at[:, span], ref_v.at[pair], ref_sem.at[pair]),
        )

    for g in range(PAIRS // 2):
        for pair in (PAIRS // 2 + g, PAIRS // 2 - 1 - g):
            for copy in load(pair):
                copy.start()

    own = jnp.concatenate([orient_ref[:, 0, :], orient_ref[:, 1, :]], axis=1).astype(F32)
    own = jnp.transpose(own) - (slab * 32).astype(F32)
    own = jnp.concatenate([own[0:64], own[64:128]], axis=1)
    for p in range(32):
        hit = jnp.where(own == float(p), 1.0, 0.0)
        counts[p:p + 1, :] = jnp.sum(hit, axis=0, keepdims=True)

    table = jnp.concatenate([ctf_ref[...], jnp.zeros((IMG, 64), F32)], axis=1)
    ctf_send[...] = table
    lane = lax.broadcasted_iota(jnp.int32, (8, 128), 1)
    near = (lane // 2 - 64).astype(F32)
    far = (lane // 2).astype(F32)
    squares = (0.5 * near * near + 0.25, 0.5 * far * far + 0.25)

    def shells(row, b):
        radius = squares[b % 2] + 0.5 * (row * row).astype(F32)
        return jnp.minimum(jnp.sqrt(radius), 63.0).astype(jnp.int32)

    def spread(slot, first, start):
        ctf_rows, square_rows = slot
        for k in range(start, 9):
            for b in range(2):
                cut = slice(b * 128, (b + 1) * 128)
                index = jnp.concatenate([shells(first + k, b)] * 8, axis=0)
                ctf = lanes(table, index)
                ctf_rows[k, :, cut] = ctf
                square_rows[k, :, cut] = (ctf * ctf).astype(BF16)

    def follow(slot, last, first):
        slot[0][0] = last[0][8]
        slot[1][0] = last[1][8]
        spread(slot, first, 1)

    def last_dims(left, right):
        return lax.dot_general(left, right, (((1,), (1,)), ((), ())), preferred_element_type=F32)

    def score(g, slot, sums):
        fit, energy = sums
        ctf_rows, square_rows = slot
        high, low = PAIRS // 2 + g, PAIRS // 2 - 1 - g
        for m in range(0, 9, 3):
            powers, squares_here = [], []
            for k in range(m, m + 3):
                power = None
                if k < 8:
                    entries = ref_v[high, :, k * 256:(k + 1) * 256]
                    power = entries * entries
                if k > 0:
                    entries = ref_v[low, :, (8 - k) * 256:(9 - k) * 256]
                    power = entries * entries if power is None else power + entries * entries
                powers.append(power)
                squares_here.append(square_rows[k])
            energy = energy + last_dims(jnp.concatenate(powers, axis=1), jnp.concatenate(squares_here, axis=1))
        for pair, mirrored in ((high, False), (low, True)):
            for n in range(2):
                t = pair * 2 + n
                for other in (True, False):
                    part = 1 - core if other else core
                    inner = pl.multiple_of(n * 2 * BLOCK + part * BLOCK, BLOCK)
                    pixels = img_v[pair, :, pl.ds(inner, BLOCK)]
                    entries = ref_v[pair, :, pl.ds(inner, BLOCK)]
                    ws = []
                    for e in range(2):
                        k = 4 * n + 2 * part + e
                        k = 8 - k if mirrored else k
                        ws.append((pixels[:, e * 256:(e + 1) * 256].astype(F32) * ctf_rows[k]).astype(BF16))
                    w = jnp.concatenate(ws, axis=1)
                    fit = fit + last_dims(entries, w)
                    if other:
                        w_send[t] = w.astype(F32)
                    else:
                        near_w[t] = w
        return fit, energy

    def twice(i, fit):
        for g in (2 * i, 2 * i + 1):
            for pair in (PAIRS // 2 + g, PAIRS // 2 - 1 - g):
                for copy in load(pair):
                    copy.wait()
        follow(slot_b, slot_a, i * 16 + 8)
        fit = score(2 * i, slot_a, fit)
        follow(slot_a, slot_b, i * 16 + 16)
        return score(2 * i + 1, slot_b, fit)

    slot_a, slot_b = (ctf_a, square_a), (ctf_b, square_b)
    spread(slot_a, jnp.int32(0), 0)
    zero = jnp.zeros((KP, IMG), F32)
    half = lax.fori_loop(0, PAIRS // 8, twice, (zero, zero))

    pl.semaphore_wait(barrier, len(peers))

    def w_copy(t):
        return pltpu.make_async_remote_copy(
            src_ref=w_send.at[t], dst_ref=w_recv.at[t], send_sem=w_ssem.at[t],
            recv_sem=w_rsem.at[t], device_id=sibling, device_id_type=MESH,
        )

    for t in range(OWNERS // 4, 3 * OWNERS // 4):
        w_copy(t).start()

    fit, energy = lax.fori_loop(PAIRS // 8, PAIRS // 4, twice, half)


    upper = lax.broadcasted_iota(jnp.int32, (KP, IMG), 0) < 32
    prior = jnp.log(jnp.where(upper, prior_ref[0], prior_ref[1]))
    value = prior + noise_ref[...] * (2.0 * fit - energy)
    count = jnp.concatenate([counts[:, 0:IMG], counts[:, IMG:2 * IMG]], axis=0)
    listed = count > 0.0
    peak = jnp.max(jnp.where(listed, value, LOWEST), axis=0, keepdims=True)
    weight = jnp.where(listed, count * jnp.exp(value - peak), 0.0)
    mass = jnp.sum(weight, axis=0, keepdims=True)
    stat_send[0:KP, 0:IMG] = weight
    stat_send[KP:KP + 1, 0:IMG] = peak
    stat_send[KP + 1:KP + 2, 0:IMG] = mass

    sent = []

    def send(src, dst, peer):
        n = len(sent)
        copy = pltpu.make_async_remote_copy(
            src_ref=src, dst_ref=dst, send_sem=ssem.at[n], recv_sem=rsem.at[n],
            device_id=peer, device_id_type=MESH,
        )
        copy.start()
        sent.append(copy)
        return copy

    stats = stat_send.at[pl.ds(KP, 8), :]
    waits = []
    for d in (2, 1, 3):
        waits.append(send(stats, stat_own.at[d - 1], (mine, (slab + d) % 4)))
        waits.append(send(stats, stat_other.at[d - 1], (flat(1 - core, x, z, y), (slab + d) % 4)))
    waits.append(send(stat_send, pair_recv, sibling))
    ctf_copy = send(ctf_send, ctf_other, sibling)

    for t in list(range(OWNERS // 4)) + list(range(3 * OWNERS // 4, OWNERS)):
        w_copy(t).start()

    order = [(2, dy, dz) for dy in (2, 1, 3, 0) for dz in (1, 0)]
    order += [(dx, dy, 1) for dx in (1, 3, 0) for dy in (2, 1, 3, 0)]
    order += [(dx, 2, 0) for dx in (1, 3, 0)]
    order += [(dx, dy, 0) for dx in (1, 3, 0) for dy in (1, 3, 0)]

    def owner(dx, dy, dz):
        return (((y + dy) % 4) * 2 + (z + dz) % 2) * 4 + (x + dx) % 4

    for copy in waits:
        copy.wait_recv()

    def share(first, second, rest):
        top = first
        for d in range(3):
            top = jnp.maximum(top, rest[d, 0:1, 0:IMG])
        total = second * jnp.exp(first - top)
        for d in range(3):
            total = total + rest[d, 1:2, 0:IMG] * jnp.exp(rest[d, 0:1, 0:IMG] - top)
        return jnp.exp(first - top) / total

    here = weight * share(peak, mass, stat_own)
    there = pair_recv[0:KP, 0:IMG] * share(pair_recv[KP:KP + 1, 0:IMG], pair_recv[KP + 1:KP + 2, 0:IMG], stat_other)
    planes = jnp.concatenate([here, there], axis=1).astype(BF16)

    def block(n):
        dx, dy, dz = order[n]
        both = jnp.concatenate([near_w[owner(dx, dy, dz)], w_recv[owner(dx, dy, dz)].astype(BF16)], axis=0)
        got = jnp.dot(planes, both, preferred_element_type=F32)
        for h in range(2):
            cut = slice(h * HALF, (h + 1) * HALF)
            for o in range(2):
                first, second = (dx, dy) if o == 0 else (dy, dx)
                for u in range(UNITS + 1):
                    row = (o * (UNITS + 1) + u) * ROWS
                    piece = got[row:row + ROWS, cut]
                    if u < UNITS:
                        part_a[o, u, h, first, second, dz] = piece
                    else:
                        part_q[o, dz, h, first, second] = piece

    def blocks(start, stop):
        for n in range(start, stop):
            w_copy(owner(*order[n])).wait_recv()
        for n in range(start, stop):
            block(n)

    f_a, g_a, h_a, d_b, z_c = {}, {}, {}, {}, {}
    z_q, f_q, g_q, h_q, d_q = {}, {}, {}, {}, {}

    def ahead(part, into, to):
        return [send(part.at[0, 2], into.at[0], to(1)), send(part.at[1, 2], into.at[1], to(3))]

    def direct(part, into, to):
        return [send(part.at[0, 3], into.at[0], to(3)), send(part.at[1, 1], into.at[1], to(1))]

    def onward(part, came, copies, into, to):
        out = []
        for h, d in ((0, 1), (1, 3)):
            copies[h].wait_recv()
            part[h, d] = part[h, d] + came[h]
            out.append(send(part.at[h, d], into.at[h], to(d)))
        return out

    def first_a(o, u):
        f_a[o, u] = ahead(part_a.at[o, u], fwd_a.at[o, u], at[o])

    def direct_a(o, u):
        g_a[o, u] = direct(part_a.at[o, u], dir_a.at[o, u], at[o])

    def second_a(o, u):
        h_a[o, u] = onward(part_a.at[o, u], fwd_a.at[o, u], f_a[o, u], sum_a.at[o, u], at[o])

    def last_a(o, u):
        for h in range(2):
            g_a[o, u][h].wait_recv()
            h_a[o, u][h].wait_recv()
            done = part_a[o, u, h, 0] + dir_a[o, u, h] + sum_a[o, u, h]
            for d in range(4):
                for dz in range(2):
                    part_b[o, u, d, dz, h] = done[d, dz]
        d_b[o, u] = [
            send(part_b.at[o, u, d], b_recv.at[o, u, d - 1], at[1 - o](d)) for d in (2, 1, 3)
        ]

    def last_b(o, u):
        for copy in d_b[o, u]:
            copy.wait_recv()
        part_b[o, u, 0] = part_b[o, u, 0] + b_recv[o, u, 0] + b_recv[o, u, 1] + b_recv[o, u, 2]
        z_c[o, u] = send(part_b.at[o, u, 0, 1], z_recv.at[o, u], at_z)

    def first_q(o):
        z_q[o].wait_recv()
        part_q[o, 0] = part_q[o, 0] + q_z[o]
        f_q[o] = ahead(part_q.at[o, 0], q_fwd.at[o], at[o])
        g_q[o] = direct(part_q.at[o, 0], q_dir.at[o], at[o])

    def second_q(o):
        h_q[o] = onward(part_q.at[o, 0], q_fwd.at[o], f_q[o], q_sum.at[o], at[o])

    def last_q(o):
        for h in range(2):
            g_q[o][h].wait_recv()
            h_q[o][h].wait_recv()
            done = part_q[o, 0, h, 0] + q_dir[o, h] + q_sum[o, h]
            for d in range(4):
                q_b[o, d, h] = done[d]
        d_q[o] = [send(q_b.at[o, d], q_recv.at[o, d - 1], at[1 - o](d)) for d in (2, 1, 3)]

    blocks(0, 8)
    for u in range(UNITS):
        first_a(0, u)
    blocks(8, 20)
    for o in range(2):
        z_q[o] = send(part_q.at[o, 1], q_z.at[o], at_z)
    blocks(20, 23)
    for u in range(UNITS):
        first_a(1, u)
    blocks(23, 32)
    for o in range(2):
        direct_a(o, 0)

    ctf_copy.wait_recv()
    squared = jnp.concatenate([ctf_ref[...], ctf_other[:, 0:SHELLS]], axis=0)
    squared = (squared * squared).astype(BF16)
    shell_sum = jnp.dot(planes, squared, preferred_element_type=F32)
    tot[0] = jnp.concatenate([shell_sum[0:32], shell_sum[32:64]], axis=1)
    tot_x = [send(tot.at[0], tot_recv.at[d - 1], at_x(d)) for d in (1, 2, 3)]

    both = (0, 1)
    for u in range(UNITS):
        for o in both:
            second_a(o, u)
        if u + 1 < UNITS:
            for o in both:
                direct_a(o, u + 1)
    for t in range(OWNERS):
        w_copy(t).wait_send()
    for copy in tot_x:
        copy.wait_recv()
    tot[1] = tot[0] + tot_recv[0] + tot_recv[1] + tot_recv[2]
    tot_y = [send(tot.at[1], tot_recv.at[d + 2], at_y(d)) for d in (1, 2, 3)]
    for o in both:
        last_a(o, 0)
    first_q(0)
    for o in both:
        last_a(o, 1)
    for copy in tot_y:
        copy.wait_recv()
    tot[2] = tot[1] + tot_recv[3] + tot_recv[4] + tot_recv[5]
    tot_z = send(tot.at[2], tot_recv.at[6], at_z)
    first_q(1)
    for o in both:
        last_a(o, 2)
    second_q(0)
    for o in both:
        last_b(o, 0)
    second_q(1)
    for o in both:
        last_b(o, 1)
    last_q(0)
    for o in both:
        last_b(o, 2)
    last_q(1)
    early = len(sent) - 40
    for copy in sent[:early]:
        copy.wait_send()

    tot_z.wait_recv()
    whole = tot[2] + tot_recv[6]
    divisors = []
    blank = jnp.zeros((32, 64), F32)
    for k in range(2):
        table_k = jnp.concatenate([whole[:, k * 64:(k + 1) * 64], blank], axis=1)
        columns = []
        for b in range(BLOCK // 128):
            row = mine * 2 + b // 2 - 64
            index = jnp.concatenate([shells(row, b)] * 4, axis=0)
            columns.append(lanes(table_k, index) + 1.0)
        divisors.append(columns)

    def finish(o, u, h, done):
        low = (o * (UNITS + 1) + u) * ROWS
        for b in range(2):
            below = divisors[o][2 * h + b][u * ROWS:(u + 1) * ROWS]
            out_ref[low:low + ROWS, pl.ds(h * HALF + b * 128, 128)] = done[:, b * 128:(b + 1) * 128] / below

    for u in range(UNITS):
        for o in range(2):
            z_c[o, u].wait_recv()
            for h in range(2):
                finish(o, u, h, part_b[o, u, 0, 0, h] + z_recv[o, u, h])
    for o in range(2):
        for copy in d_q[o]:
            copy.wait_recv()
        for h in range(2):
            finish(o, UNITS, h, q_b[o, 0, h] + q_recv[o, 0, h] + q_recv[o, 1, h] + q_recv[o, 2, h])

    for copy in sent[early:]:
        copy.wait_send()


def shards(images, references, orientations, ctf_table, inv_noise, class_weight):
    classes, planes, width = references.shape
    vmem = pl.BlockSpec(memory_space=pltpu.VMEM)
    hbm = pl.BlockSpec(memory_space=pl.ANY)
    dma = pltpu.SemaphoreType.DMA
    out = pl.pallas_call(
        kernel,
        out_shape=pltpu.VMEM((KP, BLOCK), F32),
        in_specs=[hbm, hbm, vmem, vmem, vmem, pl.BlockSpec(memory_space=pltpu.SMEM)],
        out_specs=vmem,
        scratch_shapes=[
            pltpu.VMEM((PAIRS, IMG, PAIR), BF16),
            pltpu.VMEM((PAIRS, KP, PAIR), BF16),
            pltpu.VMEM((OWNERS, IMG, BLOCK), BF16),
            pltpu.VMEM((OWNERS, IMG, BLOCK), F32),
            pltpu.VMEM((OWNERS, IMG, BLOCK), F32),
            pltpu.VMEM((9, IMG, 256), F32),
            pltpu.VMEM((9, IMG, 256), BF16),
            pltpu.VMEM((9, IMG, 256), F32),
            pltpu.VMEM((9, IMG, 256), BF16),
            pltpu.VMEM((IMG, 128), F32),
            pltpu.VMEM((IMG, 128), F32),
            pltpu.VMEM((KP + 8, 128), F32),
            pltpu.VMEM((3, 8, 128), F32),
            pltpu.VMEM((3, 8, 128), F32),
            pltpu.VMEM((KP + 8, 128), F32),
            pltpu.VMEM((2, UNITS, 2, 4, 4, 2, ROWS, HALF), F32),
            pltpu.VMEM((2, UNITS, 2, 4, 2, ROWS, HALF), F32),
            pltpu.VMEM((2, UNITS, 2, 4, 2, ROWS, HALF), F32),
            pltpu.VMEM((2, UNITS, 2, 4, 2, ROWS, HALF), F32),
            pltpu.VMEM((2, UNITS, 4, 2, 2, ROWS, HALF), F32),
            pltpu.VMEM((2, UNITS, 3, 2, 2, ROWS, HALF), F32),
            pltpu.VMEM((2, UNITS, 2, ROWS, HALF), F32),
            pltpu.VMEM((2, 2, 2, 4, 4, ROWS, HALF), F32),
            pltpu.VMEM((2, 2, 4, 4, ROWS, HALF), F32),
            pltpu.VMEM((2, 2, 4, ROWS, HALF), F32),
            pltpu.VMEM((2, 2, 4, ROWS, HALF), F32),
            pltpu.VMEM((2, 2, 4, ROWS, HALF), F32),
            pltpu.VMEM((2, 4, 2, ROWS, HALF), F32),
            pltpu.VMEM((2, 3, 2, ROWS, HALF), F32),
            pltpu.VMEM((3, 32, 128), F32),
            pltpu.VMEM((7, 32, 128), F32),
            pltpu.VMEM((32, 2 * IMG), F32),
            dma((PAIRS,)), dma((PAIRS,)), dma((OWNERS,)), dma((OWNERS,)), dma((COPIES,)), dma((COPIES,)),
        ],
        compiler_params=pltpu.CompilerParams(
            collective_id=0, has_side_effects=True, vmem_limit_bytes=60 * 2**20
        ),
        name="em_step",
    )(
        images,
        references.reshape(classes * planes, width),
        orientations,
        ctf_table,
        inv_noise.reshape(1, IMG),
        class_weight,
    )
    return out.reshape(classes, planes, BLOCK)


def solution(mesh):
    return jax.shard_map(
        shards,
        mesh=mesh,
        in_specs=(
            P("img", None),
            P(None, "slab", None),
            P("img", None, None),
            P("img", None),
            P("img"),
            P(),
        ),
        out_specs=P(None, "slab", "img"),
        check_vma=False,
    )
```
